32 devices in a mesh: lang: 8 (over z, core), batch: 4 (over y, x).
Axes of the slice: x: 2, y: 2, z: 4, core: 2. Of those that a mesh axis runs over, the one named last changes fastest.
Arguments:
- dec_states: bfloat16 [8, 48, 32, 1024], P('lang', 'batch'), may hold values from -6 to 6
- grad_out: bfloat16 [8, 48, 32, 1024], P('lang', 'batch'), may hold values from -6 to 6
- enc_rows: bfloat16 [8, 24, 128, 1024], P('lang', 'batch'), may hold values from -6 to 6
- source_lengths: int32 [8, 24], P('lang', 'batch'), may hold values from 1 to 128, as said below
- pair_counts: int32 [8, 8], replicated, may hold values from 0 to 2, as said below
- query_gain: float32 [8, 1024], P('lang'), may hold values from 0.5 to 1.5
- w_query: bfloat16 [8, 1024, 512], P('lang', 'batch'), may hold values from -0.1875 to 0.1875
- w_key: bfloat16 [8, 1024, 512], P('lang', 'batch'), may hold values from -0.1875 to 0.1875
- w_value: bfloat16 [8, 1024, 512], P('lang', 'batch'), may hold values from -0.1875 to 0.1875
- w_out: bfloat16 [8, 512, 1024], P('lang', 'batch'), may hold values from -0.25 to 0.25
Outputs:
- attended: bfloat16 [8, 48, 32, 1024], P('lang', 'batch')
- dec_grad: bfloat16 [8, 48, 32, 1024], P('lang', 'batch')
- enc_grad: bfloat16 [8, 24, 128, 1024], P('lang', 'batch')
- gain_grad: float32 [8, 1024], P('lang', 'batch')
- query_grad: float32 [8, 1024, 512], P('lang', 'batch')
- key_grad: float32 [8, 1024, 512], P('lang', 'batch')
- value_grad: float32 [8, 1024, 512], P('lang', 'batch')
- out_grad: float32 [8, 512, 1024], P('lang', 'batch')
The draws below stay inside these ranges and needn't reach their ends.
Inputs may be any that keep to these rules, and one draw needn't show every extreme that they name: `pair_counts`: each row sums to 6; a device's sentences are ordered by target language; no column sums to more than 12 and some column sums to exactly 12; no entry exceeds 2, and some entry equals it. `source_lengths`: on every device some sentence has 128 real tokens and some has 1.
All inputs are finite; a program needn't handle non-finite values.
Results may differ from the reference program's by a relative error of at most 0.02.
Values may be sent and summed in bfloat16 or wider, within the bound.
No kernel may reach another device: no remote copies, remote signals or barrier semaphores. Data moves between devices by JAX's collectives and lax.ppermute only.
A program may use at most 128 MiB of HBM per device.

```python
import jax
import jax.numpy as jnp
from jax import lax

D = 1024
HEADS = 8
HDIM = 64
SEQ = 128
TGT = 32
SENT_DEV = 6
LIVE_CAP = 12
N_LANG = 8
N_BATCH = 4


def draw_pair_counts(key, part):
    lang_total = N_LANG
    key_perm, key_delta = jax.random.split(key, 2)
    order_perm = jax.random.permutation(key_perm, lang_total)
    deltas = jax.random.randint(key_delta, (lang_total // 2,), 0, SENT_DEV + 1)
    deltas = deltas.at[0].set(SENT_DEV)
    target_loads = jnp.zeros((lang_total,), jnp.int32)
    target_loads = target_loads.at[order_perm[0::2]].set(SENT_DEV + deltas)
    target_loads = target_loads.at[order_perm[1::2]].set(SENT_DEV - deltas)
    unit_ids = jnp.arange(lang_total * SENT_DEV, dtype=jnp.int32)
    bounds = jnp.cumsum(target_loads)
    targets = jnp.sum((bounds[None, :] <= unit_ids[:, None]).astype(jnp.int32), axis=1)
    sources = unit_ids % lang_total
    return jnp.zeros((lang_total, lang_total), jnp.int32).at[sources, targets].add(1)


def draw_source_lengths(key, part):
    key_base, key_long, key_short = jax.random.split(key, 3)
    grid_shape = (N_LANG, N_BATCH, SENT_DEV)
    drawn = jax.random.randint(key_base, grid_shape, 1, SEQ + 1)
    longest = jax.random.randint(key_long, (N_LANG, N_BATCH, 1), 0, SENT_DEV)
    shortest = (longest + 1 + jax.random.randint(key_short, (N_LANG, N_BATCH, 1), 0, SENT_DEV - 1)) % SENT_DEV
    positions = jnp.arange(SENT_DEV, dtype=jnp.int32)[None, None, :]
    drawn = jnp.where(positions == longest, SEQ, drawn)
    drawn = jnp.where(positions == shortest, 1, drawn)
    return drawn.reshape(N_LANG, N_BATCH * SENT_DEV).astype(jnp.int32)


def levels(rng, dims, cuts, low, high):
    factor_of, own = 1.0, jax.random.fold_in(rng, 6)
    for position, parts in cuts:
        steps = jnp.exp(jax.random.uniform(jax.random.fold_in(own, position), (parts,), jnp.float32, low / len(cuts), high / len(cuts)))
        factor_of = factor_of * jnp.repeat(steps, dims[position] // parts).reshape([-1 if axis == position else 1 for axis in range(len(dims))])
    return factor_of


def bell_draw(rng, extent, width, limit, cuts=(), held_as=jnp.bfloat16):
    array = jax.random.normal(rng, extent, jnp.float32) * width
    if len(cuts) > 0:
        array = levels(rng, extent, cuts, -0.22, 0.18) * array
    return jnp.clip(array, min=-limit, max=limit).astype(held_as)


def setup_inputs(seed: int = 0) -> dict:
    arg_keys = jax.random.split(jax.random.key(seed), 11)
    dec_states = bell_draw(arg_keys[0], (N_LANG, N_BATCH * LIVE_CAP, TGT, D), 1.0, 6.0, ((0, 8), (1, 4)))
    grad_out = bell_draw(arg_keys[1], (N_LANG, N_BATCH * LIVE_CAP, TGT, D), 1.0, 6.0, ((0, 8), (1, 4)))
    enc_rows = bell_draw(arg_keys[2], (N_LANG, N_BATCH * SENT_DEV, SEQ, D), 1.0, 6.0, ((0, 8), (1, 4)))
    source_lengths = draw_source_lengths(jax.random.fold_in(arg_keys[10], 71), 0)
    pair_counts = draw_pair_counts(jax.random.fold_in(arg_keys[10], 71), 0)
    query_gain = jnp.clip(1.0 + 0.1 * jax.random.normal(arg_keys[5], (N_LANG, D), jnp.float32), 0.5, 1.5)
    w_query = bell_draw(arg_keys[6], (N_LANG, D, HEADS * HDIM), D ** -0.5, 0.1875, ((0, 8), (1, 4)))
    w_key = bell_draw(arg_keys[7], (N_LANG, D, HEADS * HDIM), D ** -0.5, 0.1875, ((0, 8), (1, 4)))
    w_value = bell_draw(arg_keys[8], (N_LANG, D, HEADS * HDIM), D ** -0.5, 0.1875, ((0, 8), (1, 4)))
    w_out = bell_draw(arg_keys[9], (N_LANG, HEADS * HDIM, D), (HEADS * HDIM) ** -0.5, 0.25, ((0, 8), (1, 4)))
    return dict(dec_states=dec_states, grad_out=grad_out, enc_rows=enc_rows, source_lengths=source_lengths, pair_counts=pair_counts, query_gain=query_gain, w_query=w_query, w_key=w_key, w_value=w_value, w_out=w_out)


def cross_branch(states, query_gain, w_query, w_key, w_value, w_out, memory, key_lengths):
    slot_count = states.shape[0]
    states32 = states.astype(jnp.float32)
    scale_inv = lax.rsqrt(lax.optimization_barrier(jnp.mean(states32 * states32, axis=-1, keepdims=True)) + 1e-06)
    normed = (states32 * scale_inv * query_gain).astype(jnp.bfloat16)
    queries = jnp.einsum('ktd,de->kte', normed.astype(jnp.float32), w_query.astype(jnp.float32)).astype(jnp.bfloat16)
    key_rows = jnp.einsum('ksd,de->kse', memory.astype(jnp.float32), w_key.astype(jnp.float32)).astype(jnp.bfloat16)
    value_rows = jnp.einsum('ksd,de->kse', memory.astype(jnp.float32), w_value.astype(jnp.float32)).astype(jnp.bfloat16)
    queries = queries.reshape(slot_count, queries.shape[1], HEADS, HDIM)
    key_rows = key_rows.reshape(slot_count, key_rows.shape[1], HEADS, HDIM)
    value_rows = value_rows.reshape(slot_count, value_rows.shape[1], HEADS, HDIM)
    scores = jnp.einsum('kthe,kshe->khts', queries.astype(jnp.float32), key_rows.astype(jnp.float32)) * HDIM ** (-0.5)
    key_live = jnp.arange(key_rows.shape[1], dtype=jnp.int32)[None, :] < key_lengths[:, None]
    raised = jnp.where(key_live[:, None, None, :], jnp.exp(scores), 0.0)
    empty_slot = (key_lengths == 0).astype(jnp.float32)[:, None, None, None]
    shares = (raised / (lax.optimization_barrier(jnp.sum(raised, axis=-1, keepdims=True)) + empty_slot)).astype(jnp.bfloat16)
    context = jnp.einsum('khts,kshe->kthe', shares.astype(jnp.float32), value_rows.astype(jnp.float32)).astype(jnp.bfloat16)
    context = context.reshape(slot_count, context.shape[1], HEADS * HDIM)
    return jnp.einsum('kte,ed->ktd', context.astype(jnp.float32), w_out.astype(jnp.float32))

def device_step(states, upstream, query_gain, w_query, w_key, w_value, w_out, memory, key_lengths):

    def branch_fn(states_in, gain_in, query_in, key_in, value_in, out_in, memory_in):
        return cross_branch(states_in, gain_in, query_in, key_in, value_in, out_in, memory_in, key_lengths)
    branch, backward = jax.vjp(branch_fn, states, query_gain, w_query, w_key, w_value, w_out, memory)
    gradients = backward(upstream.astype(jnp.float32))
    state_grad = (upstream.astype(jnp.float32) + gradients[0].astype(jnp.float32)).astype(jnp.bfloat16)
    return (branch.astype(jnp.bfloat16), state_grad, gradients[1:])

def reference(dec_states, grad_out, enc_rows, source_lengths, pair_counts, query_gain, w_query, w_key, w_value, w_out):
    encoded = enc_rows.reshape(N_LANG, N_BATCH, SENT_DEV, SEQ, D)
    src_lengths = source_lengths.reshape(N_LANG, N_BATCH, SENT_DEV)
    states_all = dec_states.reshape(N_LANG, N_BATCH, LIVE_CAP, TGT, D)
    upstream_all = grad_out.reshape(N_LANG, N_BATCH, LIVE_CAP, TGT, D)
    send_start = jnp.cumsum(pair_counts, axis=1) - pair_counts
    recv_start = jnp.cumsum(pair_counts, axis=0) - pair_counts
    target_loads = lax.optimization_barrier(jnp.sum(pair_counts, axis=0))
    slot_ids = jnp.arange(LIVE_CAP, dtype=jnp.int32)

    def per_device(device_id):
        target = device_id // N_BATCH
        column = device_id % N_BATCH
        column_counts = pair_counts[:, target]
        source_of = lax.optimization_barrier(jnp.sum((jnp.cumsum(column_counts)[None, :] <= slot_ids[:, None]).astype(jnp.int32), axis=1))
        source_of = jnp.minimum(source_of, N_LANG - 1).astype(jnp.int32)
        within = slot_ids - recv_start[source_of, target]
        is_valid = slot_ids < target_loads[target]
        sentence = jnp.clip(send_start[source_of, target] + within, 0, SENT_DEV - 1).astype(jnp.int32)
        memory = jnp.where(is_valid[:, None, None], encoded[source_of, column, sentence], jnp.zeros((), enc_rows.dtype))
        key_lengths = jnp.where(is_valid, src_lengths[source_of, column, sentence], 0).astype(jnp.int32)
        return device_step(states_all[target, column], upstream_all[target, column], query_gain[target], w_query[target], w_key[target], w_value[target], w_out[target], memory, key_lengths)
    branch, state_grad, gradients = lax.map(per_device, jnp.arange(N_LANG * N_BATCH, dtype=jnp.int32))
    attended = branch.reshape(N_LANG, N_BATCH * LIVE_CAP, TGT, D)
    dec_grad = state_grad.reshape(N_LANG, N_BATCH * LIVE_CAP, TGT, D)
    gain_rounded = lax.optimization_barrier(gradients[0].astype(jnp.bfloat16)).astype(jnp.float32)
    gain_grad = lax.optimization_barrier(jnp.sum(gain_rounded.reshape(N_LANG, N_BATCH, D), axis=1))
    query_grad = lax.optimization_barrier(jnp.sum(gradients[1].astype(jnp.float32).reshape(N_LANG, N_BATCH, D, HEADS * HDIM), axis=1))
    key_grad = lax.optimization_barrier(jnp.sum(gradients[2].astype(jnp.float32).reshape(N_LANG, N_BATCH, D, HEADS * HDIM), axis=1))
    value_grad = lax.optimization_barrier(jnp.sum(gradients[3].astype(jnp.float32).reshape(N_LANG, N_BATCH, D, HEADS * HDIM), axis=1))
    out_grad = lax.optimization_barrier(jnp.sum(gradients[4].astype(jnp.float32).reshape(N_LANG, N_BATCH, HEADS * HDIM, D), axis=1))
    memory_grads = gradients[5]
    sentence_ids = jnp.arange(SENT_DEV, dtype=jnp.int32)
    row_bounds = jnp.cumsum(pair_counts, axis=1)
    target_of = lax.optimization_barrier(jnp.sum((row_bounds[:, None, :] <= sentence_ids[None, :, None]).astype(jnp.int32), axis=2)).astype(jnp.int32)
    source_ids = jnp.arange(N_LANG, dtype=jnp.int32)[:, None]
    within = sentence_ids[None, :] - send_start[source_ids, target_of]
    slot_of = (recv_start[source_ids, target_of] + within).astype(jnp.int32)
    device_of = (target_of[:, None, :] * N_BATCH + jnp.arange(N_BATCH, dtype=jnp.int32)[None, :, None]).astype(jnp.int32)
    enc_grad = memory_grads[device_of, slot_of[:, None, :]]
    enc_grad = enc_grad.reshape(N_LANG, N_BATCH * SENT_DEV, SEQ, D)
    return (attended, dec_grad, enc_grad, gain_grad, query_grad, key_grad, value_grad, out_grad)
```

```python
import jax
import jax.numpy as jnp
from jax import lax
from jax.experimental import pallas as pl
from jax.experimental.pallas import tpu as pltpu
from jax.sharding import PartitionSpec as P

HEADS = 8
HDIM = 64
CORES = 2
BASE = 2
BF = jnp.bfloat16
F32 = jnp.float32
I32 = jnp.int32

SMEM = pl.BlockSpec(memory_space=pltpu.SMEM)
VMEM = pl.BlockSpec(memory_space=pltpu.VMEM)
ANY = pl.BlockSpec(memory_space=pl.ANY)


def extras(chips, most):
    spare = max(0, most - BASE)
    mid = chips // 2
    ends = tuple(1 if b in (0, chips - 1) else 0 for b in range(chips))
    inner = tuple(1 if b in (mid - 1, mid) else 0 for b in range(chips))
    tries = [(0,) * chips, inner, ends] + [(k,) * chips for k in range(1, spare + 1)]
    found = []
    for caps in tries:
        caps = tuple(min(c, spare) for c in caps)
        if caps not in found:
            found.append(caps)
    return found


class Layout:
    def __init__(self, langs, sents, live_cap):
        self.langs, self.sents, self.live_cap = langs, sents, live_cap
        self.chips = langs // CORES
        self.hops = self.chips - 1
        self.pair_cap = (live_cap + langs - 1) // langs
        most = min(CORES * self.pair_cap, sents)
        self.base = min(BASE, most)
        self.library = extras(self.chips, most)
        self.more = max(max(c) for c in self.library)
        self.runs = [(0, self.base)] + [(self.base + k, 1) for k in range(self.more)]
        flows = self.hops * (self.base + self.more)
        self.send = 1
        self.take_piece = self.send + flows
        self.take_index = self.take_piece + live_cap
        self.take_from = self.take_index + live_cap
        self.take_sent = self.take_from + live_cap
        self.take_live = self.take_sent + live_cap
        self.back_piece = self.take_live + live_cap
        self.back_index = self.back_piece + flows
        self.home_piece = self.back_index + flows
        self.home_index = self.home_piece + sents
        self.size = self.home_index + sents

    def packs(self):
        return [n for _, n in self.runs for _ in range(self.hops)]

    def packed(self):
        place = 0
        for first, n in self.runs:
            for e in range(1, self.hops + 1):
                for k in range(n):
                    yield place, e, first + k
                    place += 1


def make_plan(pair_counts, me, lay):
    langs, chips, sents = lay.langs, lay.chips, lay.sents

    def body(who, c, out, ss, rs, need, total):
        me = who[0]
        chip, core = me // CORES, me % CORES

        def rows(s, _):
            acc = I32(0)
            for t in range(langs):
                ss[s, t] = acc
                acc = acc + c[s, t]
            return 0

        lax.fori_loop(0, langs, rows, 0)

        def cols(t, _):
            acc = I32(0)
            for s in range(langs):
                rs[s, t] = acc
                acc = acc + c[s, t]
            return 0

        lax.fori_loop(0, langs, cols, 0)

        def needs(b, _):
            top = I32(0)
            for s in range(langs):
                n = c[s, b * CORES] + c[s, b * CORES + 1]
                top = jnp.maximum(top, jnp.where(b == s // CORES, 0, n))
            need[b] = top
            return 0

        lax.fori_loop(0, chips, needs, 0)
        choice = I32(len(lay.library) - 1)
        for i in reversed(range(len(lay.library) - 1)):
            ok = need[0] <= lay.base + lay.library[i][0]
            for b in range(1, chips):
                ok = jnp.logical_and(ok, need[b] <= lay.base + lay.library[i][b])
            choice = jnp.where(ok, i, choice)
        out[0] = choice
        for b in range(chips):
            extra = I32(lay.library[-1][b])
            for i in range(len(lay.library) - 1):
                extra = jnp.where(choice == i, lay.library[i][b], extra)
            total[b] = lay.base + extra

        def run(s, b):
            return jnp.minimum(ss[s, b * CORES], sents - total[b])

        def run_of(slot):
            which = jnp.where(slot < lay.base, 0, slot - lay.base + 1)
            return which, jnp.where(slot < lay.base, slot, 0)

        for place, e, k in lay.packed():
            goal = (chip + e) % chips
            out[lay.send + place] = jnp.clip(run(me, goal) + k, 0, sents - 1)
            source = (chip - e + chips) % chips * CORES + core
            j = run(source, chip) + k
            t = chip * CORES + (j >= ss[source, chip * CORES + 1]).astype(I32)
            out[lay.back_piece + place] = (t != me).astype(I32)
            out[lay.back_index + place] = jnp.clip(
                rs[source, t] + j - ss[source, t], 0, lay.live_cap - 1
            )
        for k in range(lay.live_cap):
            for table in (lay.take_piece, lay.take_index, lay.take_from, lay.take_sent, lay.take_live):
                out[table + k] = I32(0)

        def takes(s, _):
            for i in range(lay.pair_cap):

                @pl.when(i < c[s, me])
                def _():
                    k = rs[s, me] + i
                    sent = ss[s, me] + i
                    hop = (chip - s // CORES + chips) % chips
                    which, offset = run_of(sent - run(s, chip))
                    away = 2 + 2 * (which * lay.hops + hop - 1)
                    other = (s % CORES != core).astype(I32)
                    out[lay.take_piece + k] = jnp.where(hop == 0, 0, away) + other
                    out[lay.take_index + k] = jnp.where(hop == 0, sent, offset)
                    out[lay.take_from + k] = s
                    out[lay.take_sent + k] = sent
                    out[lay.take_live + k] = I32(1)

            return 0

        lax.fori_loop(0, langs, takes, 0)

        def homes(t, _):
            for i in range(lay.pair_cap):

                @pl.when(i < c[me, t])
                def _():
                    j = ss[me, t] + i
                    goal = t // CORES
                    hop = (goal - chip + chips) % chips
                    which, offset = run_of(j - run(me, goal))
                    out[lay.home_piece + j] = jnp.where(
                        hop == 0, (t != me).astype(I32), 2 + which * lay.hops + hop - 1
                    )
                    out[lay.home_index + j] = jnp.where(hop == 0, rs[me, t] + i, offset)

            return 0

        lax.fori_loop(0, langs, homes, 0)

    return pl.pallas_call(
        body,
        out_shape=jax.ShapeDtypeStruct((lay.size,), I32),
        in_specs=[SMEM, SMEM],
        out_specs=SMEM,
        scratch_shapes=[
            pltpu.SMEM((langs, langs), I32),
            pltpu.SMEM((langs, langs), I32),
            pltpu.SMEM((chips,), I32),
            pltpu.SMEM((chips,), I32),
        ],
        name="plan",
    )(me[None].astype(I32), pair_counts)


def block_gather(table, piece_at, index_at, pieces, groups, name):
    total = sum(groups)
    block = pieces[0].shape[1:]
    count = len(pieces)

    def body(table_ref, *refs):
        ins, outs, sem = refs[:count], refs[count:-1], refs[-1]
        base = 0
        for g, size in enumerate(groups):
            for r in range(size):
                i = base + r
                for p in range(count):
                    copy = pltpu.make_async_copy(
                        ins[p].at[table_ref[index_at + i]], outs[g].at[r], sem.at[i]
                    )
                    if count == 1:
                        copy.start()
                    else:
                        pl.when(table_ref[piece_at + i] == p)(copy.start)
            base += size
        base = 0
        for g, size in enumerate(groups):
            for r in range(size):
                pltpu.make_async_copy(ins[0].at[0], outs[g].at[r], sem.at[base + r]).wait()
            base += size

    return pl.pallas_call(
        body,
        out_shape=[jax.ShapeDtypeStruct((size,) + block, pieces[0].dtype) for size in groups],
        in_specs=[SMEM] + [ANY] * count,
        out_specs=[VMEM] * len(groups),
        scratch_shapes=[pltpu.SemaphoreType.DMA((total,))],
        name=name,
    )(table, *pieces)


def assemble(pieces, row, deep, wide):
    count = len(pieces)

    def body(row_ref, *refs):
        ins, (q, k, v, o), sem = refs[:count], refs[count:-1], refs[-1]

        def copies(i, p):
            ref = ins[p]
            for w, out in enumerate((q, k, v)):
                yield pltpu.make_async_copy(
                    ref.at[w], out.at[pl.ds(i * deep[0], deep[0])], sem.at[i, w]
                )
            for h in range(2):
                yield pltpu.make_async_copy(
                    ref.at[3, pl.ds(h * wide[0], wide[0])],
                    o.at[pl.ds(i * wide[0], wide[0]), pl.ds(h * deep[1], deep[1])],
                    sem.at[i, 3 + h],
                )

        for i in range(count):
            for p in range(count):

                @pl.when(row_ref[0] ^ i == p)
                def _():
                    for c in copies(i, p):
                        c.start()

        for i in range(count):
            for c in copies(i, 0):
                c.wait()

    tall = jax.ShapeDtypeStruct((count * deep[0], deep[1]), BF)
    return pl.pallas_call(
        body,
        out_shape=[tall, tall, tall, jax.ShapeDtypeStruct((count * wide[0], wide[1]), BF)],
        in_specs=[pl.BlockSpec(memory_space=pltpu.SMEM)]
        + [pl.BlockSpec(memory_space=pl.ANY)] * count,
        out_specs=[pl.BlockSpec(memory_space=pltpu.VMEM)] * 4,
        scratch_shapes=[pltpu.SemaphoreType.DMA((count, 5))],
    )(row[None].astype(jnp.int32), *pieces)


def dot(a, b, ca, cb):
    return lax.dot_general(a, b, (((ca,), (cb,)), ((), ())), preferred_element_type=F32)


def attend(table, lengths, pieces, w_key, w_value, queries, context_grad, lay, tgt):
    count = len(pieces)
    seq, width = pieces[0].shape[1:]
    inner = w_key.shape[1]
    slots = lay.live_cap
    group = next(g for g in (4, 3, 2, 1) if slots % g == 0)

    def body(table_ref, len_ref, *refs):
        ins = refs[:count]
        wk, wv, q_ref, g_ref, mem, dmem, dk, dv, dq, ctx, keys, values, sem = refs[count:]

        def start(i, _):
            for p in range(count):

                @pl.when(table_ref[lay.take_piece + i] == p)
                def _():
                    pltpu.make_async_copy(
                        ins[p].at[table_ref[lay.take_index + i]],
                        mem.at[pl.ds(pl.multiple_of(i * seq, seq), seq)],
                        sem.at[i],
                    ).start()

            return 0

        lax.fori_loop(0, slots, start, 0)
        for n in range(slots // group):
            for i in range(n * group, (n + 1) * group):
                pltpu.make_async_copy(
                    ins[0].at[0], mem.at[pl.ds(i * seq, seq)], sem.at[i]
                ).wait()
            span = pl.ds(n * group * seq, group * seq)
            block = mem[span, :]
            keys[span, :] = dot(block, wk[...], 1, 0).astype(BF)
            values[span, :] = dot(block, wv[...], 1, 0).astype(BF)

        full = HEADS * tgt
        own = (
            lax.broadcasted_iota(I32, (full, inner), 0) // tgt
            == lax.broadcasted_iota(I32, (full, inner), 1) // HDIM
        )
        own_head = [
            lax.broadcasted_iota(I32, (tgt, inner), 1) // HDIM == h for h in range(HEADS)
        ]
        column = lax.broadcasted_iota(I32, (full, seq), 1)
        zero = jnp.zeros((), BF)

        def spread(x):
            return jnp.where(own, jnp.concatenate([x] * HEADS, axis=0), zero)

        def collect(x):
            out = jnp.where(own_head[0], x[:tgt], 0.0)
            for h in range(1, HEADS):
                out = jnp.where(own_head[h], x[h * tgt : (h + 1) * tgt], out)
            return out.astype(BF)

        def slot(i, _):
            here = pl.ds(pl.multiple_of(i * seq, seq), seq)
            mine = pl.ds(pl.multiple_of(i * tgt, tgt), tgt)
            live = table_ref[lay.take_live + i]
            length = live * len_ref[table_ref[lay.take_from + i], table_ref[lay.take_sent + i]]
            empty = jnp.where(length == 0, 1.0, 0.0)
            k, v = keys[here, :], values[here, :]
            q, g = spread(q_ref[mine, :]), spread(g_ref[mine, :])
            scores = dot(q, k, 1, 1) * HDIM ** (-0.5)
            raised = jnp.where(column < length, jnp.exp(scores), 0.0)
            exact = raised / (jnp.sum(raised, axis=1, keepdims=True) + empty)
            shares = exact.astype(BF)
            ctx[mine, :] = collect(dot(shares, v, 1, 0))
            up = dot(g, v, 1, 1).astype(BF).astype(F32)
            mean = jnp.sum(exact * up, axis=1, keepdims=True)
            ds = (exact * (up - mean) * HDIM ** (-0.5)).astype(BF)
            dq[mine, :] = collect(dot(ds, k, 1, 0))
            dk[here, :] = dot(ds, q, 0, 0).astype(BF)
            dv[here, :] = dot(shares, g, 0, 0).astype(BF)
            return 0

        lax.fori_loop(0, slots, slot, 0)
        for n in range(slots // group):
            span = pl.ds(n * group * seq, group * seq)
            dmem[span, :] = (
                dot(dk[span, :], wk[...], 1, 1) + dot(dv[span, :], wv[...], 1, 1)
            ).astype(BF)

    shape = jax.ShapeDtypeStruct
    return pl.pallas_call(
        body,
        out_shape=[
            shape((slots * seq, width), BF),
            shape((slots * seq, width), BF),
            shape((slots * seq, inner), BF),
            shape((slots * seq, inner), BF),
            shape((slots * tgt, inner), BF),
            shape((slots * tgt, inner), BF),
        ],
        in_specs=[SMEM, SMEM] + [ANY] * count + [VMEM] * 4,
        out_specs=[VMEM] * 6,
        scratch_shapes=[
            pltpu.VMEM((slots * seq, inner), BF),
            pltpu.VMEM((slots * seq, inner), BF),
            pltpu.SemaphoreType.DMA((slots,)),
        ],
        compiler_params=pltpu.CompilerParams(vmem_limit_bytes=48 << 20),
        name="attend",
    )(table, lengths, *pieces, w_key, w_value, queries, context_grad)


def partner(x):
    size = lax.axis_size("lang")
    return lax.ppermute(x, "lang", [(i, i ^ 1) for i in range(size)])


def per_device(
    dec_states,
    grad_out,
    enc_rows,
    source_lengths,
    pair_counts,
    query_gain,
    w_query,
    w_key,
    w_value,
    w_out,
):
    langs = lax.axis_size("lang")
    batch = lax.axis_size("batch")
    me = lax.axis_index("lang")
    row = lax.axis_index("batch")
    sents, seq, width = enc_rows.shape[1:]
    live_cap, tgt = dec_states.shape[1:3]
    lay = Layout(langs, sents, live_cap)
    chips, hops = lay.chips, lay.hops
    runs = len(lay.runs)

    table = make_plan(pair_counts, me, lay)
    choice = table[0]

    rows = enc_rows[0]
    sends = block_gather(table, None, lay.send, [rows], lay.packs(), "pack_rows")

    def shift(e, sign, last):
        return [
            (c * CORES + k, (c + sign * e) % chips * CORES + k)
            for c in range(chips)
            for k in range(CORES)
            if last[(c + sign * e) % chips if sign > 0 else c]
        ]

    def used(caps, u):
        return tuple(u == 0 or c >= u for c in caps)

    def fetch(caps):
        def go(lengths, *sends):
            got = []
            for u in range(runs):
                for e in range(1, hops + 1):
                    out = sends[u * hops + e - 1]
                    if any(used(caps, u)):
                        out = lax.ppermute(out, "lang", shift(e, 1, used(caps, u)))
                    got.append(out)
            mates = [
                partner(x) if any(used(caps, n // hops)) else x for n, x in enumerate(got)
            ]
            lengths, got[0] = lax.optimization_barrier((lengths, got[0]))
            lengths = lax.all_to_all(
                jnp.broadcast_to(lengths, (langs, sents)), "lang", 0, 0, tiled=True
            )
            return tuple(got), tuple(mates), lengths

        return go

    deep, wide = w_query.shape[1:], w_out.shape[1:]
    packed = jnp.stack(
        [
            w_query[0],
            w_key[0],
            w_value[0],
            jnp.concatenate([w_out[0, :, : deep[1]], w_out[0, :, deep[1] :]], axis=0),
        ]
    )
    shards = [packed] + [
        lax.ppermute(packed, "batch", [(i, i ^ g) for i in range(batch)]) for g in range(1, batch)
    ]
    mate_rows = partner(rows)
    if len(lay.library) > 1:
        fetched = lax.switch(
            choice, [fetch(c) for c in lay.library], source_lengths, *sends
        )
    else:
        fetched = fetch(lay.library[0])(source_lengths, *sends)
    got, mates, all_lengths = fetched
    pieces = [rows, mate_rows]
    for a, b in zip(got, mates):
        pieces += [a, b]

    full_query, full_key, full_value, full_out = assemble(shards, row, deep, wide)
    states = dec_states[0].reshape(live_cap * tgt, width)
    upstream = grad_out[0].reshape(live_cap * tgt, width)

    def norm(x, gain):
        x32 = x.astype(F32)
        inverse = lax.rsqrt(jnp.mean(x32 * x32, axis=-1, keepdims=True) + 1e-06)
        return (x32 * inverse * gain).astype(BF)

    normed, norm_back = jax.vjp(norm, states, query_gain[0])
    queries = dot(normed, full_query, 1, 0).astype(BF)
    context_grad = dot(upstream, full_out, 1, 1).astype(BF)
    memory, memory_grad, key_part, value_part, query_row_grad, context = attend(
        table, all_lengths, pieces, full_key, full_value, queries, context_grad, lay, tgt
    )

    blocks = memory_grad.reshape(live_cap, seq, width)
    mate_blocks = partner(blocks)
    packs = block_gather(
        table, lay.back_piece, lay.back_index, [blocks, mate_blocks], lay.packs(), "pack_grads"
    )
    back = [
        lax.ppermute(packs[e - 1], "lang", shift(e, -1, (1,) * chips))
        for e in range(1, hops + 1)
    ]

    key_part = dot(memory, key_part, 0, 0).astype(BF)
    value_part = dot(memory, value_part, 0, 0).astype(BF)
    query_part = dot(normed, query_row_grad, 0, 0).astype(BF)
    out_part = dot(context, upstream, 0, 0).astype(BF)
    normed_grad = dot(query_row_grad, full_query, 1, 1).astype(BF)
    state_part, gain_part = norm_back(normed_grad)
    (query_part, key_part, value_part, out_part, gain_part), _ = lax.optimization_barrier(
        ((query_part, key_part, value_part, out_part, gain_part), packs)
    )

    def block_of(part, i):
        size = part.shape[0] // batch
        return lax.dynamic_slice_in_dim(part, i * size, size, 0)

    gain_rows = 16
    gain_size = width // batch

    def outgoing(i):
        low = block_of(out_part, i)
        gain = block_of(gain_part.astype(BF), i)
        gain = jnp.pad(gain[None], ((0, gain_rows - 1), (0, deep[1] - gain_size)))
        return jnp.concatenate(
            [
                block_of(query_part, i),
                block_of(key_part, i),
                block_of(value_part, i),
                low[:, : deep[1]],
                low[:, deep[1] :],
                gain,
            ],
            axis=0,
        )

    parts = [outgoing(row ^ g) for g in range(batch)]
    got = [
        lax.ppermute(parts[g], "batch", [(i, i ^ g) for i in range(batch)])
        for g in range(1, batch)
    ]

    def give_more(caps):
        def go(*packs):
            out = []
            for u in range(1, runs):
                for e in range(1, hops + 1):
                    x = packs[(u - 1) * hops + e - 1]
                    if any(used(caps, u)):
                        x = lax.ppermute(x, "lang", shift(e, -1, used(caps, u)))
                    out.append(x)
            return tuple(out)

        return go

    if len(lay.library) > 1:
        late, _ = lax.optimization_barrier((tuple(packs[hops:]), tuple(parts)))
        back += lax.switch(choice, [give_more(c) for c in lay.library], *late)
    enc_grad = block_gather(
        table,
        lay.home_piece,
        lay.home_index,
        [blocks, mate_blocks] + back,
        [sents],
        "home_grads",
    )[0]

    attended = dot(context, full_out, 1, 0).astype(BF)
    dec_grad = (upstream.astype(F32) + state_part.astype(F32)).astype(BF)
    summed = parts[0].astype(F32)
    for x in got:
        summed = summed + x.astype(F32)
    d, w = deep[0], wide[0]
    out_sum = jnp.concatenate([summed[3 * d : 3 * d + w], summed[3 * d + w : 3 * d + 2 * w]], axis=1)
    return (
        attended.reshape(dec_states.shape),
        dec_grad.reshape(dec_states.shape),
        enc_grad[None],
        summed[3 * d + 2 * w, :gain_size][None],
        summed[:d][None],
        summed[d : 2 * d][None],
        summed[2 * d : 3 * d][None],
        out_sum[None],
    )


def solution(mesh):
    wide = P("lang", "batch", None, None)
    weight = P("lang", "batch", None)
    return jax.shard_map(
        per_device,
        mesh=mesh,
        in_specs=(
            wide,
            wide,
            wide,
            P("lang", "batch"),
            P(),
            P("lang", None),
            weight,
            weight,
            weight,
            weight,
        ),
        out_specs=(wide, wide, wide, P("lang", "batch"), weight, weight, weight, weight),
        check_vma=False,
    )
```

```python
import jax
import jax.numpy as jnp
from jax import lax
from jax.experimental import pallas as pl
from jax.experimental.pallas import tpu as pltpu
from jax.sharding import PartitionSpec as P


HEADS = 8
HDIM = 64
CORES = 2
BASE = 2
BF = jnp.bfloat16
F32 = jnp.float32
I32 = jnp.int32

SMEM = pl.BlockSpec(memory_space=pltpu.SMEM)
VMEM = pl.BlockSpec(memory_space=pltpu.VMEM)
ANY = pl.BlockSpec(memory_space=pl.ANY)


def extras(chips, most):
    spare = max(0, most - BASE)
    mid = chips // 2
    ends = tuple(1 if b in (0, chips - 1) else 0 for b in range(chips))
    inner = tuple(1 if b in (mid - 1, mid) else 0 for b in range(chips))
    tries = [(0,) * chips, inner, ends] + [(k,) * chips for k in range(1, spare + 1)]
    found = []
    for caps in tries:
        caps = tuple(min(c, spare) for c in caps)
        if caps not in found:
            found.append(caps)
    return found


class Layout:
    def __init__(self, langs, sents, live_cap):
        self.langs, self.sents, self.live_cap = langs, sents, live_cap
        self.chips = langs // CORES
        self.hops = self.chips - 1
        self.pair_cap = (live_cap + langs - 1) // langs
        most = min(CORES * self.pair_cap, sents)
        self.base = min(BASE, most)
        self.library = extras(self.chips, most)
        self.more = max(max(c) for c in self.library)
        self.runs = [(0, self.base)] + [(self.base + k, 1) for k in range(self.more)]
        flows = self.hops * (self.base + self.more)
        self.send = 1
        self.take_piece = self.send + flows
        self.take_index = self.take_piece + live_cap
        self.take_from = self.take_index + live_cap
        self.take_sent = self.take_from + live_cap
        self.take_live = self.take_sent + live_cap
        self.back_piece = self.take_live + live_cap
        self.back_index = self.back_piece + flows
        self.home_piece = self.back_index + flows
        self.home_index = self.home_piece + sents
        self.size = self.home_index + sents

    def packs(self):
        return [n for _, n in self.runs for _ in range(self.hops)]

    def packed(self):
        place = 0
        for first, n in self.runs:
            for e in range(1, self.hops + 1):
                for k in range(n):
                    yield place, e, first + k
                    place += 1


def make_plan(pair_counts, me, lay):
    langs, chips, sents = lay.langs, lay.chips, lay.sents

    def body(who, c, out, ss, rs, need, total):
        me = who[0]
        chip, core = me // CORES, me % CORES

        def rows(s, _):
            acc = I32(0)
            for t in range(langs):
                ss[s, t] = acc
                acc = acc + c[s, t]
            return 0

        lax.fori_loop(0, langs, rows, 0)

        def cols(t, _):
            acc = I32(0)
            for s in range(langs):
                rs[s, t] = acc
                acc = acc + c[s, t]
            return 0

        lax.fori_loop(0, langs, cols, 0)

        def needs(b, _):
            top = I32(0)
            for s in range(langs):
                n = c[s, b * CORES] + c[s, b * CORES + 1]
                top = jnp.maximum(top, jnp.where(b == s // CORES, 0, n))
            need[b] = top
            return 0

        lax.fori_loop(0, chips, needs, 0)
        choice = I32(len(lay.library) - 1)
        for i in reversed(range(len(lay.library) - 1)):
            ok = need[0] <= lay.base + lay.library[i][0]
            for b in range(1, chips):
                ok = jnp.logical_and(ok, need[b] <= lay.base + lay.library[i][b])
            choice = jnp.where(ok, i, choice)
        out[0] = choice
        for b in range(chips):
            extra = I32(lay.library[-1][b])
            for i in range(len(lay.library) - 1):
                extra = jnp.where(choice == i, lay.library[i][b], extra)
            total[b] = lay.base + extra

        def run(s, b):
            return jnp.minimum(ss[s, b * CORES], sents - total[b])

        def run_of(slot):
            which = jnp.where(slot < lay.base, 0, slot - lay.base + 1)
            return which, jnp.where(slot < lay.base, slot, 0)

        for place, e, k in lay.packed():
            goal = (chip + e) % chips
            out[lay.send + place] = jnp.clip(run(me, goal) + k, 0, sents - 1)
            source = (chip - e + chips) % chips * CORES + core
            j = run(source, chip) + k
            t = chip * CORES + (j >= ss[source, chip * CORES + 1]).astype(I32)
            out[lay.back_piece + place] = (t != me).astype(I32)
            out[lay.back_index + place] = jnp.clip(
                rs[source, t] + j - ss[source, t], 0, lay.live_cap - 1
            )
        for k in range(lay.live_cap):
            for table in (lay.take_piece, lay.take_index, lay.take_from, lay.take_sent, lay.take_live):
                out[table + k] = I32(0)

        def takes(s, _):
            for i in range(lay.pair_cap):

                @pl.when(i < c[s, me])
                def _():
                    k = rs[s, me] + i
                    sent = ss[s, me] + i
                    hop = (chip - s // CORES + chips) % chips
                    which, offset = run_of(sent - run(s, chip))
                    away = 2 + 2 * (which * lay.hops + hop - 1)
                    other = (s % CORES != core).astype(I32)
                    out[lay.take_piece + k] = jnp.where(hop == 0, 0, away) + other
                    out[lay.take_index + k] = jnp.where(hop == 0, sent, offset)
                    out[lay.take_from + k] = s
                    out[lay.take_sent + k] = sent
                    out[lay.take_live + k] = I32(1)

            return 0

        lax.fori_loop(0, langs, takes, 0)

        def homes(t, _):
            for i in range(lay.pair_cap):

                @pl.when(i < c[me, t])
                def _():
                    j = ss[me, t] + i
                    goal = t // CORES
                    hop = (goal - chip + chips) % chips
                    which, offset = run_of(j - run(me, goal))
                    out[lay.home_piece + j] = jnp.where(
                        hop == 0, (t != me).astype(I32), 2 + which * lay.hops + hop - 1
                    )
                    out[lay.home_index + j] = jnp.where(hop == 0, rs[me, t] + i, offset)

            return 0

        lax.fori_loop(0, langs, homes, 0)

    return pl.pallas_call(
        body,
        out_shape=jax.ShapeDtypeStruct((lay.size,), I32),
        in_specs=[SMEM, SMEM],
        out_specs=SMEM,
        scratch_shapes=[
            pltpu.SMEM((langs, langs), I32),
            pltpu.SMEM((langs, langs), I32),
            pltpu.SMEM((chips,), I32),
            pltpu.SMEM((chips,), I32),
        ],
        name="plan",
    )(me[None].astype(I32), pair_counts)


def block_gather(table, piece_at, index_at, pieces, groups):
    total = sum(groups)
    block = pieces[0].shape[1:]
    count = len(pieces)

    def body(table_ref, *refs):
        ins, outs, sem = refs[:count], refs[count:-1], refs[-1]
        base = 0
        for g, size in enumerate(groups):
            for r in range(size):
                i = base + r
                for p in range(count):
                    copy = pltpu.make_async_copy(
                        ins[p].at[table_ref[index_at + i]], outs[g].at[r], sem.at[i]
                    )
                    if count == 1:
                        copy.start()
                    else:
                        pl.when(table_ref[piece_at + i] == p)(copy.start)
            base += size
        base = 0
        for g, size in enumerate(groups):
            for r in range(size):
                pltpu.make_async_copy(ins[0].at[0], outs[g].at[r], sem.at[base + r]).wait()
            base += size

    return pl.pallas_call(
        body,
        out_shape=[jax.ShapeDtypeStruct((size,) + block, pieces[0].dtype) for size in groups],
        in_specs=[SMEM] + [ANY] * count,
        out_specs=[VMEM] * len(groups),
        scratch_shapes=[pltpu.SemaphoreType.DMA((total,))],
    )(table, *pieces)


def assemble(pieces, row, deep, wide):
    count = len(pieces)

    def body(row_ref, *refs):
        ins, (q, k, v, o), sem = refs[:count], refs[count:-1], refs[-1]

        def copies(i, p):
            ref = ins[p]
            for w, out in enumerate((q, k, v)):
                yield pltpu.make_async_copy(
                    ref.at[w], out.at[pl.ds(i * deep[0], deep[0])], sem.at[i, w]
                )
            for h in range(2):
                yield pltpu.make_async_copy(
                    ref.at[3, pl.ds(h * wide[0], wide[0])],
                    o.at[pl.ds(i * wide[0], wide[0]), pl.ds(h * deep[1], deep[1])],
                    sem.at[i, 3 + h],
                )

        for i in range(count):
            for p in range(count):

                @pl.when(row_ref[0] ^ i == p)
                def _():
                    for c in copies(i, p):
                        c.start()

        for i in range(count):
            for c in copies(i, 0):
                c.wait()

    tall = jax.ShapeDtypeStruct((count * deep[0], deep[1]), BF)
    return pl.pallas_call(
        body,
        out_shape=[tall, tall, tall, jax.ShapeDtypeStruct((count * wide[0], wide[1]), BF)],
        in_specs=[pl.BlockSpec(memory_space=pltpu.SMEM)]
        + [pl.BlockSpec(memory_space=pl.ANY)] * count,
        out_specs=[pl.BlockSpec(memory_space=pltpu.VMEM)] * 4,
        scratch_shapes=[pltpu.SemaphoreType.DMA((count, 5))],
    )(row[None].astype(jnp.int32), *pieces)


def dot(a, b, ca, cb):
    return lax.dot_general(a, b, (((ca,), (cb,)), ((), ())), preferred_element_type=F32)


def attend(table, lengths, pieces, w_key, w_value, queries, context_grad, lay, tgt):
    count = len(pieces)
    seq, width = pieces[0].shape[1:]
    inner = w_key.shape[1]
    slots = lay.live_cap
    group = next(g for g in (4, 3, 2, 1) if slots % g == 0)

    def body(table_ref, len_ref, *refs):
        ins = refs[:count]
        wk, wv, q_ref, g_ref, mem, dmem, dk, dv, dq, ctx, keys, values, sem = refs[count:]

        def start(i, _):
            for p in range(count):

                @pl.when(table_ref[lay.take_piece + i] == p)
                def _():
                    pltpu.make_async_copy(
                        ins[p].at[table_ref[lay.take_index + i]],
                        mem.at[pl.ds(pl.multiple_of(i * seq, seq), seq)],
                        sem.at[i],
                    ).start()

            return 0

        lax.fori_loop(0, slots, start, 0)
        for n in range(slots // group):
            for i in range(n * group, (n + 1) * group):
                pltpu.make_async_copy(
                    ins[0].at[0], mem.at[pl.ds(i * seq, seq)], sem.at[i]
                ).wait()
            span = pl.ds(n * group * seq, group * seq)
            block = mem[span, :]
            keys[span, :] = dot(block, wk[...], 1, 0).astype(BF)
            values[span, :] = dot(block, wv[...], 1, 0).astype(BF)

        full = HEADS * tgt
        own = (
            lax.broadcasted_iota(I32, (full, inner), 0) // tgt
            == lax.broadcasted_iota(I32, (full, inner), 1) // HDIM
        )
        own_head = [
            lax.broadcasted_iota(I32, (tgt, inner), 1) // HDIM == h for h in range(HEADS)
        ]
        column = lax.broadcasted_iota(I32, (full, seq), 1)
        zero = jnp.zeros((), BF)

        def spread(x):
            return jnp.where(own, jnp.concatenate([x] * HEADS, axis=0), zero)

        def collect(x):
            out = jnp.where(own_head[0], x[:tgt], 0.0)
            for h in range(1, HEADS):
                out = jnp.where(own_head[h], x[h * tgt : (h + 1) * tgt], out)
            return out.astype(BF)

        def slot(i, _):
            here = pl.ds(pl.multiple_of(i * seq, seq), seq)
            mine = pl.ds(pl.multiple_of(i * tgt, tgt), tgt)
            live = table_ref[lay.take_live + i]
            length = live * len_ref[table_ref[lay.take_from + i], table_ref[lay.take_sent + i]]
            empty = jnp.where(length == 0, 1.0, 0.0)
            k, v = keys[here, :], values[here, :]
            q, g = spread(q_ref[mine, :]), spread(g_ref[mine, :])
            scores = dot(q, k, 1, 1) * HDIM ** (-0.5)
            raised = jnp.where(column < length, jnp.exp(scores), 0.0)
            exact = raised / (jnp.sum(raised, axis=1, keepdims=True) + empty)
            shares = exact.astype(BF)
            ctx[mine, :] = collect(dot(shares, v, 1, 0))
            up = dot(g, v, 1, 1).astype(BF).astype(F32)
            mean = jnp.sum(exact * up, axis=1, keepdims=True)
            ds = (exact * (up - mean) * HDIM ** (-0.5)).astype(BF)
            dq[mine, :] = collect(dot(ds, k, 1, 0))
            dk[here, :] = dot(ds, q, 0, 0).astype(BF)
            dv[here, :] = dot(shares, g, 0, 0).astype(BF)
            return 0

        lax.fori_loop(0, slots, slot, 0, unroll=group)
        for n in range(slots // group):
            span = pl.ds(n * group * seq, group * seq)
            dmem[span, :] = (
                dot(dk[span, :], wk[...], 1, 1) + dot(dv[span, :], wv[...], 1, 1)
            ).astype(BF)

    shape = jax.ShapeDtypeStruct
    return pl.pallas_call(
        body,
        out_shape=[
            shape((slots * seq, width), BF),
            shape((slots * seq, width), BF),
            shape((slots * seq, inner), BF),
            shape((slots * seq, inner), BF),
            shape((slots * tgt, inner), BF),
            shape((slots * tgt, inner), BF),
        ],
        in_specs=[SMEM, SMEM] + [ANY] * count + [VMEM] * 4,
        out_specs=[VMEM] * 6,
        scratch_shapes=[
            pltpu.VMEM((slots * seq, inner), BF),
            pltpu.VMEM((slots * seq, inner), BF),
            pltpu.SemaphoreType.DMA((slots,)),
        ],
        compiler_params=pltpu.CompilerParams(vmem_limit_bytes=48 << 20),
        name="attend",
    )(table, lengths, *pieces, w_key, w_value, queries, context_grad)


def blanks(count, shape):
    return pl.pallas_call(
        lambda *refs: None,
        out_shape=[jax.ShapeDtypeStruct(shape, BF)] * count,
        out_specs=[ANY] * count,
        name="blanks",
    )()


def partner(x):
    size = lax.axis_size("lang")
    return lax.ppermute(x, "lang", [(i, i ^ 1) for i in range(size)])


def per_device(
    dec_states,
    grad_out,
    enc_rows,
    source_lengths,
    pair_counts,
    query_gain,
    w_query,
    w_key,
    w_value,
    w_out,
):
    langs = lax.axis_size("lang")
    batch = lax.axis_size("batch")
    me = lax.axis_index("lang")
    row = lax.axis_index("batch")
    sents, seq, width = enc_rows.shape[1:]
    live_cap, tgt = dec_states.shape[1:3]
    lay = Layout(langs, sents, live_cap)
    chips, hops = lay.chips, lay.hops

    table = make_plan(pair_counts, me, lay)
    choice = table[0]

    rows = enc_rows[0]
    flows = lay.hops * lay.base
    sends = block_gather(table, None, lay.send, [rows], lay.packs()[:hops])
    if lay.more:
        sends += block_gather(table, None, lay.send + flows, [rows], lay.packs()[hops:])

    def shift(e, sign, last):
        return [
            (c * CORES + k, (c + sign * e) % chips * CORES + k)
            for c in range(chips)
            for k in range(CORES)
            if last[(c + sign * e) % chips if sign > 0 else c]
        ]

    def used(caps, u):
        return tuple(u == 0 or c >= u for c in caps)

    def fetch(caps):
        def go(*sends):
            live = [any(used(caps, 1 + n // hops)) for n in range(len(sends))]
            got, mates = list(sends), list(sends)
            if not all(live):
                spare = iter(blanks(2 * live.count(False), sends[0].shape))
            for n, x in enumerate(sends):
                if live[n]:
                    got[n] = lax.ppermute(
                        x, "lang", shift(1 + n % hops, 1, used(caps, 1 + n // hops))
                    )
                else:
                    got[n], mates[n] = next(spare), next(spare)
            for n in range(len(sends)):
                if live[n]:
                    mates[n] = partner(got[n])
            return tuple(got), tuple(mates)

        return go

    deep, wide = w_query.shape[1:], w_out.shape[1:]
    packed = jnp.stack(
        [
            w_query[0],
            w_key[0],
            w_value[0],
            jnp.concatenate([w_out[0, :, : deep[1]], w_out[0, :, deep[1] :]], axis=0),
        ]
    )
    shards = [packed] + [
        lax.ppermute(packed, "batch", [(i, i ^ g) for i in range(batch)])
        for g in range(1, batch)
    ]
    mate_rows = partner(rows)
    got = [
        lax.ppermute(sends[e - 1], "lang", shift(e, 1, (1,) * chips))
        for e in range(1, hops + 1)
    ]
    mates = [partner(x) for x in got]
    all_lengths = lax.all_to_all(
        jnp.broadcast_to(source_lengths, (langs, sents)), "lang", 0, 0, tiled=True
    )
    shards, all_lengths = lax.optimization_barrier((shards, all_lengths))
    if lay.more:
        late, mate_late = lax.switch(
            choice, [fetch(c) for c in lay.library], *sends[hops:]
        )
        got, mates = got + list(late), mates + list(mate_late)
    pieces = [rows, mate_rows]
    for a, b in zip(got, mates):
        pieces += [a, b]

    full_query, full_key, full_value, full_out = assemble(shards, row, deep, wide)
    states = dec_states[0].reshape(live_cap * tgt, width)
    upstream = grad_out[0].reshape(live_cap * tgt, width)

    def norm(x, gain):
        x32 = x.astype(F32)
        inverse = lax.rsqrt(jnp.mean(x32 * x32, axis=-1, keepdims=True) + 1e-06)
        return (x32 * inverse * gain).astype(BF)

    normed, norm_back = jax.vjp(norm, states, query_gain[0])
    queries = dot(normed, full_query, 1, 0).astype(BF)
    context_grad = dot(upstream, full_out, 1, 1).astype(BF)
    memory, memory_grad, key_part, value_part, query_row_grad, context = attend(
        table, all_lengths, pieces, full_key, full_value, queries, context_grad, lay, tgt
    )

    blocks = memory_grad.reshape(live_cap, seq, width)
    mate_blocks = partner(blocks)
    packs = block_gather(table, lay.back_piece, lay.back_index, [blocks, mate_blocks], lay.packs())
    back = [
        lax.ppermute(packs[e - 1], "lang", shift(e, -1, (1,) * chips))
        for e in range(1, hops + 1)
    ]

    def block_of(part, i):
        size = part.shape[0] // batch
        return lax.dynamic_slice_in_dim(part, i * size, size, 0)

    gain_rows = 16
    gain_size = width // batch

    def first_parts(i):
        low = block_of(out_part, i)
        gain = block_of(gain_part.astype(BF), i)
        gain = jnp.pad(gain[None], ((0, gain_rows - 1), (0, deep[1] - gain_size)))
        return jnp.concatenate(
            [block_of(query_part, i), low[:, : deep[1]], low[:, deep[1] :], gain], axis=0
        )

    def second_parts(i):
        return jnp.concatenate([block_of(key_part, i), block_of(value_part, i)], axis=0)

    def exchange(parts):
        return [
            lax.ppermute(parts[g], "batch", [(i, i ^ g) for i in range(batch)])
            for g in range(1, batch)
        ]

    query_part = dot(normed, query_row_grad, 0, 0).astype(BF)
    out_part = dot(context, upstream, 0, 0).astype(BF)
    normed_grad = dot(query_row_grad, full_query, 1, 1).astype(BF)
    state_part, gain_part = norm_back(normed_grad)
    key_part = dot(memory, key_part, 0, 0).astype(BF)
    value_part = dot(memory, value_part, 0, 0).astype(BF)
    parts_a = [first_parts(row ^ g) for g in range(batch)]
    got_a = exchange(parts_a)
    parts_b = [second_parts(row ^ g) for g in range(batch)]
    got_b = exchange(parts_b)

    def give_more(caps):
        def go(*packs):
            live = [any(used(caps, 1 + n // hops)) for n in range(len(packs))]
            out = list(packs)
            if not all(live):
                spare = iter(blanks(live.count(False), packs[0].shape))
            for n, x in enumerate(packs):
                if live[n]:
                    out[n] = lax.ppermute(
                        x, "lang", shift(1 + n % hops, -1, used(caps, 1 + n // hops))
                    )
                else:
                    out[n] = next(spare)
            return tuple(out)

        return go

    if lay.more:
        late = tuple(packs[hops:])
        back += lax.switch(choice, [give_more(c) for c in lay.library], *late)
    enc_grad = block_gather(
        table, lay.home_piece, lay.home_index, [blocks, mate_blocks] + back, [sents]
    )[0]

    attended = dot(context, full_out, 1, 0).astype(BF)
    dec_grad = (upstream.astype(F32) + state_part.astype(F32)).astype(BF)

    def total_of(own, others):
        total = own.astype(F32)
        for x in others:
            total = total + x.astype(F32)
        return total

    d, w = deep[0], wide[0]
    first, second = total_of(parts_a[0], got_a), total_of(parts_b[0], got_b)
    out_sum = jnp.concatenate([first[d : d + w], first[d + w : d + 2 * w]], axis=1)
    return (
        attended.reshape(dec_states.shape),
        dec_grad.reshape(dec_states.shape),
        enc_grad[None],
        first[d + 2 * w, :gain_size][None],
        first[:d][None],
        second[:d][None],
        second[d : 2 * d][None],
        out_sum[None],
    )


def solution(mesh):
    wide = P("lang", "batch", None, None)
    weight = P("lang", "batch", None)

    return jax.shard_map(
        per_device,
        mesh=mesh,
        in_specs=(
            wide,
            wide,
            wide,
            P("lang", "batch"),
            P(),
            P("lang", None),
            weight,
            weight,
            weight,
            weight,
        ),
        out_specs=(wide, wide, wide, P("lang", "batch"), weight, weight, weight, weight),
        check_vma=False,
    )
```
